32 devices in a mesh: ens: 2 (over y), lat: 4 (over x, core), lon: 4 (over z).
Axes of the slice: x: 2, y: 2, z: 4, core: 2. Of those that a mesh axis runs over, the one named last changes fastest.
Arguments:
- tokens: bfloat16 [176, 44, 1024], P(('ens', 'lat'), 'lon'), parts along dimension 0, may hold values from -6 to 6
- qkv_weight: bfloat16 [2, 1024, 1280], P(None, None, 'lon'), may hold values from -4 to 4
- out_weight: bfloat16 [2, 1024, 1024], P(None, None, 'lon'), may hold values from -0.1875 to 0.1875
- norm_gain: float32 [2, 1024], replicated, may hold values from 0.5 to 1.5
- conv_weight: bfloat16 [9, 1024], replicated, may hold values from -4 to 4
- conv_bias: bfloat16 [1024], replicated, may hold values from -6 to 6
Outputs:
- result: bfloat16 [176, 44, 1024], P(('ens', 'lat'), 'lon'), parts along dimension 0
The draws below stay inside these ranges and needn't reach their ends.
There are 2 independent parts, one for each index of `ens`. The reference program is written for one: setup_inputs(seed, part) draws one part's arguments, and reference() takes and returns one part's arrays. A program takes and returns all parts, laid end to end along the dimension named above; an argument that names none is the same for every part. Nothing has to cross between parts.
All inputs are finite; a program needn't handle non-finite values.
Results may differ from the reference program's by a relative error of at most 0.04.
Values may be sent and summed in bfloat16 or wider, within the bound.
A program may use at most 64 MiB of HBM per device.

```python
import jax
import jax.numpy as jnp
from jax import lax

D = 1024
HEADS = 16
KV = 2
HD = 64
QKV = 1280
LATS = 88
LONS = 44


def draw_qkv_weight(key, part):
    normal_base = jnp.clip(jax.random.normal(key, (2, D, QKV), jnp.float32), -6.0, 6.0) * D ** (-0.5)
    return normal_base.astype(jnp.bfloat16)


def block_levels(key, dims, shards, smallest, top_value):
    loudness = 1.0
    for dim, parts in shards:
        heights = jax.random.uniform(jax.random.fold_in(jax.random.fold_in(key, 6), dim), (parts,), jnp.float32, smallest / len(shards), top_value / len(shards))
        loudness = loudness * jnp.repeat(jnp.exp(heights), dims[dim] // parts).reshape((-1,) + (1,) * (len(dims) - 1 - dim))
    return loudness


def bell_draw(stream_key, shape, width, most, cuts=(), kind=jnp.bfloat16):
    array = jax.random.normal(stream_key, shape, jnp.float32) * width
    if len(cuts) > 0:
        array = block_levels(stream_key, shape, cuts, -0.22, 0.18) * array
    return jnp.clip(array, min=-most, max=most).astype(kind)


def setup_inputs(seed: int = 0, part: int = 0) -> dict:
    key_of = jax.random.split(jax.random.key(seed), 7)
    own_keys = jax.random.split(jax.random.fold_in(key_of[6], part), 7)
    tokens = bell_draw(own_keys[0], (LATS, LONS, D), 1.0, 6.0, ((0, 4), (1, 4)))
    qkv_weight = draw_qkv_weight(jax.random.fold_in(key_of[6], 71), part)
    out_weight = bell_draw(key_of[2], (2, D, D), D ** -0.5, 0.1875, ((2, 4),))
    norm_gain = jnp.clip(1.0 + 0.1 * jax.random.normal(key_of[3], (2, D), jnp.float32), 0.5, 1.5)
    conv_weight = bell_draw(key_of[4], (9, D), 0.3, 4.0)
    conv_bias = bell_draw(key_of[5], (D,), 0.5, 6.0)
    return {"tokens": tokens, "qkv_weight": qkv_weight, "out_weight": out_weight, "norm_gain": norm_gain, "conv_weight": conv_weight, "conv_bias": conv_bias}


def split_keyval(keyval):
    batch, length, columns = keyval.shape
    keys = keyval[..., :KV * HD].reshape(batch, length, KV, HD)
    values = keyval[..., KV * HD:].reshape(batch, length, KV, HD)
    return (keys, values)

def attend_lines(query, keyval):
    batch, length, feature = query.shape
    keys, values = split_keyval(keyval)
    grouped = query.reshape(batch, length, KV, HEADS // KV, HD)
    scores = jnp.einsum('nqgjd,nkgd->ngjqk', grouped.astype(jnp.float32), keys.astype(jnp.float32)) * HD ** (-0.5)
    peak = lax.optimization_barrier(jnp.max(scores, axis=-1, keepdims=True))
    expon = jnp.exp(scores - peak)
    denominator = lax.optimization_barrier(jnp.sum(expon, axis=-1))
    weights = expon.astype(jnp.bfloat16)
    mixed = jnp.einsum('ngjqk,nkgd->nqgjd', weights.astype(jnp.float32), values.astype(jnp.float32))
    mixed = mixed / jnp.transpose(denominator, (0, 3, 1, 2))[..., None]
    return mixed.reshape(batch, length, feature).astype(jnp.bfloat16)

def attend_single(line_pair):
    query, keyval = line_pair
    return attend_lines(query[None], keyval[None])[0]

def rms_norm(current, gain):
    values = current.astype(jnp.float32)
    scaled = values * lax.rsqrt(lax.optimization_barrier(jnp.mean(values * values, axis=-1, keepdims=True)) + 1e-06)
    return (scaled * gain.astype(jnp.float32)).astype(jnp.bfloat16)

def reference(tokens, qkv_weight, out_weight, norm_gain, conv_weight, conv_bias):
    lat_rows, lon_cols, feature = tokens.shape
    values = tokens.astype(jnp.float32)
    padded = jnp.pad(values, ((1, 1), (0, 0), (0, 0)))
    padded = jnp.concatenate([padded[:, -1:], padded, padded[:, :1]], axis=1)
    total = values + conv_bias.astype(jnp.float32)
    for shift_lat in range(3):
        for shift_lon in range(3):
            total = total + conv_weight[3 * shift_lat + shift_lon].astype(jnp.float32) * padded[shift_lat:shift_lat + lat_rows, shift_lon:shift_lon + lon_cols]
    current = total.astype(jnp.bfloat16)
    for section_index in range(2):
        normed = rms_norm(current, norm_gain[section_index])
        projected = jnp.dot(normed.reshape(-1, feature), qkv_weight[section_index], preferred_element_type=jnp.float32)
        projected = projected.astype(jnp.bfloat16).reshape(lat_rows, lon_cols, -1)
        if section_index == 0:
            attended = lax.map(attend_single, (projected[..., :feature], projected[..., feature:]))
        else:
            turned = jnp.transpose(projected, (1, 0, 2))
            attended = lax.map(attend_single, (turned[..., :feature], turned[..., feature:]))
            attended = jnp.transpose(attended, (1, 0, 2))
        output = jnp.dot(attended.reshape(-1, feature), out_weight[section_index], preferred_element_type=jnp.float32)
        current = (current.astype(jnp.float32) + output.reshape(lat_rows, lon_cols, feature)).astype(jnp.bfloat16)
    return current
```

```python
import functools

import jax
import jax.numpy as jnp
from jax import lax
from jax.experimental import pallas as pl
from jax.experimental.pallas import tpu as pltpu
from jax.sharding import PartitionSpec as P

HEADS = 16
KV = 2
HD = 64


def with_halo(cells, sides, width, closed):
    for axis, dim in sides:
        count = lax.axis_size(axis)
        ends = count if closed else count - 1
        head = lax.slice_in_dim(cells, 0, width, axis=dim)
        tail = lax.slice_in_dim(cells, cells.shape[dim] - width, cells.shape[dim], axis=dim)
        cells = jnp.concatenate(
            [
                lax.ppermute(tail, axis, [(i, (i + 1) % count) for i in range(ends)]),
                cells,
                lax.ppermute(head, axis, [((i + 1) % count, i) for i in range(ends)]),
            ],
            axis=dim,
        )
    return cells


def split_keyval(keyval):
    batch, length, columns = keyval.shape
    keys = keyval[..., : KV * HD].reshape(batch, length, KV, HD)
    values = keyval[..., KV * HD :].reshape(batch, length, KV, HD)
    return (keys, values)


def line_scores(query, keys):
    batch, length, feature = query.shape
    grouped = query.reshape(batch, length, KV, HEADS // KV, HD)
    return jnp.einsum(
        "nqgjd,nkgd->ngjqk", grouped, keys, preferred_element_type=jnp.float32
    ) * HD ** (-0.5)


def attend_lines(query, keyval):
    batch, length, feature = query.shape
    keys, values = split_keyval(keyval)
    scores = line_scores(query, keys)
    peak = jnp.max(scores, axis=-1, keepdims=True)
    expon = jnp.exp(scores - peak)
    denominator = jnp.sum(expon, axis=-1)
    mixed = jnp.einsum(
        "ngjqk,nkgd->nqgjd", expon.astype(jnp.bfloat16), values, preferred_element_type=jnp.float32
    )
    mixed = mixed / jnp.transpose(denominator, (0, 3, 1, 2))[..., None]
    return mixed.reshape(batch, length, feature).astype(jnp.bfloat16)


def rms_norm(current, gain):
    values = current.astype(jnp.float32)
    scaled = values * lax.rsqrt(jnp.mean(values * values, axis=-1, keepdims=True) + 1e-06)
    return (scaled * gain).astype(jnp.bfloat16)


def shards(tokens, qkv_weight, out_weight, norm_gain, conv_weight, conv_bias):
    lat_rows, lon_cols, feature = tokens.shape
    widened = with_halo(tokens, (("lon", 1),), 1, True)
    padded = with_halo(widened, (("lat", 0),), 1, False)
    total = tokens.astype(jnp.float32) + conv_bias.astype(jnp.float32)
    for shift_lat in range(3):
        for shift_lon in range(3):
            window = padded[
                shift_lat : shift_lat + lat_rows, shift_lon : shift_lon + lon_cols
            ].astype(jnp.float32)
            total = total + conv_weight[3 * shift_lat + shift_lon].astype(jnp.float32) * window
    current = total.astype(jnp.bfloat16)
    for section_index in range(2):
        weight_in, weight_out = (
            lax.all_gather(qkv_weight[section_index], "lon", axis=1, tiled=True),
            lax.all_gather(out_weight[section_index], "lon", axis=1, tiled=True),
        )
        normed = rms_norm(current, norm_gain[section_index])
        projected = jnp.dot(
            normed.reshape(-1, feature), weight_in, preferred_element_type=jnp.float32
        )
        projected = projected.astype(jnp.bfloat16).reshape(lat_rows, lon_cols, -1)
        query = projected[..., :feature]
        keyval = projected[..., feature:]
        if section_index == 0:
            gathered = lax.all_gather(keyval, "lon", axis=1, tiled=True)
            attended = attend_lines(query, gathered)
        else:
            gathered = lax.all_gather(keyval, "lat", axis=0, tiled=True)
            attended = attend_lines(
                jnp.transpose(query, (1, 0, 2)), jnp.transpose(gathered, (1, 0, 2))
            )
            attended = jnp.transpose(attended, (1, 0, 2))
        output = jnp.dot(
            attended.reshape(-1, feature), weight_out, preferred_element_type=jnp.float32
        )
        current = (
            current.astype(jnp.float32) + output.reshape(lat_rows, lon_cols, feature)
        ).astype(jnp.bfloat16)
    return current


MESH = pl.DeviceIdType.MESH
F32 = jnp.float32
BF16 = jnp.bfloat16
PLANE = 8


def remote(src, dst, send, recv, device):
    return pltpu.make_async_remote_copy(
        src_ref=src, dst_ref=dst, send_sem=send, recv_sem=recv, device_id=device, device_id_type=MESH
    )


def step_kernel(
    nlat, nlon, tokens, wq_in, wo_in, gain, conv_w, conv_b, out,
    wq, wo, pad, colf, col, hcol, hrow, hcor, cur, normed, proj, att, kv0, kv1,
    sem_w, sem_z, sem_f, sem_c, sem_hs, sem_hr, sem_ks, sem_kr, sem_l,
):
    rows, cols, feature = tokens.shape
    step0, step1 = 16, 32
    count = rows * step0
    ens, lat, lon = lax.axis_index("ens"), lax.axis_index("lat"), lax.axis_index("lon")
    here = ens * 4 + lax.rem(lat, 4)

    def flip(value, bit):
        return value + bit - 2 * bit * lax.rem(value // bit, 2)

    piece = feature // PLANE
    dev_core = (ens, flip(lat, 1), lon)
    dev_x = (ens, flip(lat, 2), lon)
    dev_y = (1 - ens, lat, lon)
    dev_xy = (1 - ens, flip(lat, 2), lon)
    p_core, p_x, p_y = flip(here, 1), flip(here, 2), flip(here, 4)
    p_xy = flip(p_x, 4)
    far = [lax.rem(lon + d, nlon) for d in range(nlon)]
    farlat = [lax.rem(lat + d, nlat) for d in range(nlat)]

    def part(m, s, p):
        buf = wo if m % 2 else wq
        return buf.at[m // 2, s, pl.ds(pl.multiple_of(p * piece, piece), piece), :]

    def own(m):
        return (wo_in if m % 2 else wq_in).at[m // 2]

    barrier = pltpu.get_barrier_semaphore()
    greet = [(ens, lat, far[d]) for d in range(1, nlon)]
    greet += [(ens, farlat[d], lon) for d in range(1, nlat)]
    greet += [(ens, farlat[a], far[b]) for a in (1, nlat - 1) for b in (1, nlon - 1)]
    greet += [dev_y, dev_xy]
    for device in greet:
        pl.semaphore_signal(barrier, inc=1, device_id=device, device_id_type=MESH)
    pl.semaphore_wait(barrier, len(greet))

    pending, kv_sends = [], []

    def launch(copy):
        copy.start()
        pending.append(copy)

    def send_z(m):
        for d in range(1, nlon):
            launch(remote(
                own(m).at[pl.ds(pl.multiple_of(here * piece, piece), piece), :],
                part(m, lon, here), sem_z.at[m, d], sem_w.at[m, lon, here], (ens, lat, far[d]),
            ))

    def arrived(m, s, p):
        remote(part(m, s, p), part(m, s, p), sem_z.at[m, 0], sem_w.at[m, s, p], dev_core).wait_recv()

    def pass_on(m, s, p, send, device):
        launch(remote(part(m, s, p), part(m, s, p), send, sem_w.at[m, s, p], device))

    def spread(m):
        for d in (1, 3, 2) if nlon == 4 else range(1, nlon):
            arrived(m, far[d], here)
            pass_on(m, far[d], here, sem_f.at[m, d, 0], dev_x)
            pass_on(m, far[d], here, sem_f.at[m, d, 1], dev_y)
            pass_on(m, far[d], here, sem_f.at[m, d, 2], dev_xy)
            pass_on(m, far[d], here, sem_f.at[m, d, 3], dev_core)

    def share(m):
        for d in (1, 3, 2) if nlon == 4 else range(1, nlon):
            for k, p in enumerate((p_x, p_y, p_xy)):
                arrived(m, far[d], p)
                pass_on(m, far[d], p, sem_c.at[m, d, k], dev_core)

    def finish(m):
        pltpu.make_async_copy(own(m), (wo if m % 2 else wq).at[m // 2, lon], sem_l.at[m]).wait()
        for d in range(1, nlon):
            for p in (p_core, flip(p_x, 1), flip(p_y, 1), flip(p_xy, 1)):
                arrived(m, far[d], p)

    send_z(0)
    for m in range(4):
        pltpu.make_async_copy(own(m), (wo if m % 2 else wq).at[m // 2, lon], sem_l.at[m]).start()

    colf[...] = jnp.zeros_like(colf)
    for i in range(rows):
        row = tokens[i].astype(F32)
        pad[1 + i, 8 : 8 + cols, :] = row
        colf[0, i : i + 1, :] = row[0:1]
        colf[1, i : i + 1, :] = row[cols - 1 : cols]
    col[...] = colf[...].astype(BF16)
    low, high = pl.ds(0, 16), pl.ds(16, 16)
    north, south, west, east = farlat[nlat - 1], farlat[1], far[nlon - 1], far[1]
    halos = [
        (col.at[1], hcol.at[0], (ens, lat, east)),
        (col.at[0], hcol.at[1], (ens, lat, west)),
        (tokens.at[rows - 1], hrow.at[0], (ens, south, lon)),
        (tokens.at[0], hrow.at[1], (ens, north, lon)),
        (col.at[1, high], hcor.at[0], (ens, south, east)),
        (col.at[0, high], hcor.at[1], (ens, south, west)),
        (col.at[1, low], hcor.at[2], (ens, north, east)),
        (col.at[0, low], hcor.at[3], (ens, north, west)),
    ]
    hcopies = [remote(a, b, sem_hs.at[k], sem_hr.at[k], dev) for k, (a, b, dev) in enumerate(halos)]
    for copy in hcopies:
        launch(copy)
    for m in (1, 2, 3):
        send_z(m)
    spread(0)
    for copy in hcopies:
        copy.wait_recv()

    for side, place in ((0, 7), (1, 8 + cols)):
        edge = hcol[side].astype(F32)
        for i in range(rows):
            pad[1 + i, place : place + 1, :] = edge[i : i + 1]
    last = rows - 1 - 16
    for k, (index, inside) in enumerate(((0, lat > 0), (rows + 1, lat < nlat - 1))):
        keep = jnp.where(inside, 1.0, 0.0).astype(F32)
        pick = last if k == 0 else 0
        pad[index, 8 : 8 + cols, :] = hrow[k].astype(F32) * keep
        pad[index, 7:8, :] = hcor[2 * k].astype(F32)[pick : pick + 1] * keep
        pad[index, 8 + cols : 9 + cols, :] = hcor[2 * k + 1].astype(F32)[pick : pick + 1] * keep

    taps = conv_w[...].astype(F32)
    bias = conv_b[...].astype(F32)
    alive = lax.broadcasted_iota(jnp.int32, (step0, 1), 0) < cols

    def rms(values, k):
        scaled = values * lax.rsqrt(jnp.mean(values * values, axis=-1, keepdims=True) + 1e-06)
        return (scaled * gain[k : k + 1, :]).astype(BF16)

    def conv_row(i, carry):
        total = pad[i + 1, 8 : 8 + step0, :] + bias
        for a in range(3):
            for b in range(3):
                total = total + taps[3 * a + b : 3 * a + b + 1] * pad[i + a, 7 + b : 7 + b + step0, :]
        rounded = jnp.where(alive, total, 0.0).astype(BF16)
        spot = pl.ds(pl.multiple_of(i * step0, step0), step0)
        cur[spot, :] = rounded
        normed[spot, :] = rms(rounded.astype(F32), 0)
        return carry

    lax.fori_loop(0, rows, conv_row, 0)

    def halves(pair_block):
        left = lax.broadcasted_iota(jnp.int32, pair_block.shape, 1) < HD
        swapped = jnp.concatenate([pair_block[:, HD:], pair_block[:, :HD]], axis=1)
        zero = jnp.zeros_like(pair_block)
        first = (jnp.where(left, pair_block, zero), jnp.where(left, zero, swapped))
        second = (jnp.where(left, swapped, zero), jnp.where(left, zero, pair_block))
        return (first, second)

    def attend(kv, parts, blocks, step, valid):
        width = parts * step
        pairs = HEADS // KV // 2

        def body(r, carry):
            spot = pl.ds(pl.multiple_of(r * step, step), step)
            keys = jnp.concatenate([kv[s, spot, 0 : KV * HD] for s in range(parts)], axis=0)
            values = jnp.concatenate([kv[s, spot, KV * HD :] for s in range(parts)], axis=0)
            kh, vh = halves(keys), halves(values)
            lane = lax.broadcasted_iota(jnp.int32, (1, width), 1)
            valid_key = lax.rem(lane, step) < valid
            left = lax.broadcasted_iota(jnp.int32, (1, 2 * HD), 1) < HD
            for g in range(KV):
                base = g * pairs
                query = jnp.concatenate(
                    [proj[spot, (base + p) * 128 : (base + p + 1) * 128] for p in range(pairs)], axis=0
                )
                mixed, inverse = None, []
                for half in range(2):
                    scores = lax.dot_general(
                        query, kh[g][half], (((1,), (1,)), ((), ())), preferred_element_type=F32
                    ) * HD ** (-0.5)
                    scores = jnp.where(valid_key, scores, -jnp.inf)
                    expon = jnp.exp(scores - jnp.max(scores, axis=-1, keepdims=True))
                    inverse.append(1.0 / jnp.sum(expon, axis=-1, keepdims=True))
                    term = jnp.dot(expon.astype(BF16), vh[g][half], preferred_element_type=F32)
                    mixed = term if mixed is None else mixed + term
                mixed = (mixed * jnp.where(left, inverse[0], inverse[1])).astype(BF16)
                for p in range(pairs):
                    att[spot, (base + p) * 128 : (base + p + 1) * 128] = mixed[p * step : (p + 1) * step]
            return carry

        lax.fori_loop(0, blocks, body, 0)

    def project(k, which):
        for t in which:
            both = [
                jnp.dot(normed[...], wq[k, s], preferred_element_type=F32).astype(BF16)
                for s in (2 * t, 2 * t + 1)
            ]
            width = both[0].shape[1]
            proj[:, 2 * t * width : 2 * (t + 1) * width] = jnp.concatenate(both, axis=1)

    def send_kv(k, kv, targets, mine):
        for d, device in targets:
            copy = remote(
                proj.at[:, pl.ds(feature, 2 * KV * HD)], kv.at[mine], sem_ks.at[k, d], sem_kr.at[k, mine], device
            )
            copy.start()
            kv_sends.append(copy)
        kv[mine] = proj[:, feature:]

    def take_kv(k, kv, sources):
        for s in sources:
            remote(kv.at[s], kv.at[s], sem_ks.at[k, 0], sem_kr.at[k, s], dev_core).wait_recv()

    def back(k, values, s, width):
        lanes = pl.ds(s * width, width)
        return (cur[:, lanes].astype(F32) + jnp.dot(values, wo[k, s], preferred_element_type=F32)).astype(BF16)

    share(0)
    spread(1)
    finish(0)
    project(0, (1,))
    send_kv(0, kv0, [(d, (ens, lat, far[d])) for d in range(1, nlon)], lon)
    project(0, (0,))
    share(1)
    spread(2)
    take_kv(0, kv0, far[1:])
    attend(kv0, nlon, rows, step0, cols)
    finish(1)
    width = wo.shape[3]
    for s in range(nlon):
        cur[:, s * width : (s + 1) * width] = back(0, att[...], s, width)
    share(2)
    spread(3)

    def norm_row(i, carry):
        spot = pl.ds(pl.multiple_of(i * step1, step1), step1)
        att[spot, :] = rms(cur[spot, :].astype(F32), 1)
        return carry

    lax.fori_loop(0, count // step1, norm_row, 0)
    to = lax.broadcasted_iota(jnp.int32, (count, count), 0)
    fro = lax.broadcasted_iota(jnp.int32, (count, count), 1)
    turn = (fro == lax.rem(to, step1) * step0 + to // step1) & (lax.rem(to, step1) < rows)
    normed[...] = jnp.dot(turn.astype(F32).astype(BF16), att[...], preferred_element_type=F32).astype(BF16)
    for copy in kv_sends:
        copy.wait_send()
    finish(2)
    project(1, (1,))
    send_kv(1, kv1, [(d, (ens, farlat[d], lon)) for d in range(1, nlat)], lat)
    project(1, (0,))
    share(3)
    take_kv(1, kv1, farlat[1:])
    attend(kv1, nlat, cols, step1, rows)
    unturn = (fro == lax.rem(to, step0) * step1 + to // step0) & (lax.rem(to, step0) < cols)
    normed[...] = jnp.dot(unturn.astype(F32).astype(BF16), att[...], preferred_element_type=F32).astype(BF16)
    finish(3)
    for s in range(nlon):
        done = back(1, normed[...], s, width)
        out[:, :, s * width : (s + 1) * width] = done.reshape(rows, step0, width)[:, :cols, :]
    for copy in pending + kv_sends[nlon - 1 :]:
        copy.wait_send()


def fused(tokens, qkv_weight, out_weight, norm_gain, conv_weight, conv_bias, nlat, nlon):
    rows, cols, feature = tokens.shape
    count = rows * 16
    vmem = pl.BlockSpec(memory_space=pltpu.VMEM)
    hbm = pl.BlockSpec(memory_space=pl.ANY)
    dma = pltpu.SemaphoreType.DMA
    return pl.pallas_call(
        functools.partial(step_kernel, nlat, nlon),
        out_shape=jax.ShapeDtypeStruct(tokens.shape, BF16),
        in_specs=[vmem, hbm, hbm, vmem, vmem, vmem],
        out_specs=vmem,
        scratch_shapes=[
            pltpu.VMEM((2, nlon) + qkv_weight.shape[1:], BF16),
            pltpu.VMEM((2, nlon) + out_weight.shape[1:], BF16),
            pltpu.VMEM((rows + 2, 32, feature), F32),
            pltpu.VMEM((2, 32, feature), F32),
            pltpu.VMEM((2, 32, feature), BF16),
            pltpu.VMEM((2, 32, feature), BF16),
            pltpu.VMEM((2, cols, feature), BF16),
            pltpu.VMEM((4, 16, feature), BF16),
            pltpu.VMEM((count, feature), BF16),
            pltpu.VMEM((count, feature), BF16),
            pltpu.VMEM((count, feature + 2 * KV * HD), BF16),
            pltpu.VMEM((count, feature), BF16),
            pltpu.VMEM((nlon, count, 2 * KV * HD), BF16),
            pltpu.VMEM((nlat, count, 2 * KV * HD), BF16),
            dma((4, nlon, PLANE)),
            dma((4, nlon)),
            dma((4, nlon, 4)),
            dma((4, nlon, 3)),
            dma((8,)),
            dma((8,)),
            dma((2, max(nlat, nlon))),
            dma((2, max(nlat, nlon))),
            dma((4,)),
        ],
        compiler_params=pltpu.CompilerParams(
            collective_id=0, has_side_effects=True, vmem_limit_bytes=56 * 2**20
        ),
    )(tokens, qkv_weight, out_weight, norm_gain, conv_weight, conv_bias.reshape(1, feature))


def entry(tokens, qkv_weight, out_weight, norm_gain, conv_weight, conv_bias):
    nens, nlat, nlon = (lax.axis_size(name) for name in ("ens", "lat", "lon"))
    if (nens, nlat, nlon) == (2, 4, 4) and tokens.shape[:2] == (22, 11):
        return fused(
            tokens, qkv_weight, out_weight, norm_gain, conv_weight, conv_bias, nlat, nlon
        )
    return shards(tokens, qkv_weight, out_weight, norm_gain, conv_weight, conv_bias)


def solution(mesh):
    in_specs = (
        P(("ens", "lat"), "lon", None),
        P(None, None, "lon"),
        P(None, None, "lon"),
        P(),
        P(),
        P(),
    )
    out_specs = P(("ens", "lat"), "lon", None)
    return jax.shard_map(entry, mesh=mesh, in_specs=in_specs, out_specs=out_specs, check_vma=False)
```

```python
import functools

import jax
import jax.numpy as jnp
from jax import lax
from jax.experimental import pallas as pl
from jax.experimental.pallas import tpu as pltpu
from jax.sharding import PartitionSpec as P

HEADS = 16
KV = 2
HD = 64


def with_halo(cells, sides, width, closed):
    for axis, dim in sides:
        count = lax.axis_size(axis)
        ends = count if closed else count - 1
        head = lax.slice_in_dim(cells, 0, width, axis=dim)
        tail = lax.slice_in_dim(cells, cells.shape[dim] - width, cells.shape[dim], axis=dim)
        cells = jnp.concatenate(
            [
                lax.ppermute(tail, axis, [(i, (i + 1) % count) for i in range(ends)]),
                cells,
                lax.ppermute(head, axis, [((i + 1) % count, i) for i in range(ends)]),
            ],
            axis=dim,
        )
    return cells


def split_keyval(keyval):
    batch, length, columns = keyval.shape
    keys = keyval[..., : KV * HD].reshape(batch, length, KV, HD)
    values = keyval[..., KV * HD :].reshape(batch, length, KV, HD)
    return (keys, values)


def line_scores(query, keys):
    batch, length, feature = query.shape
    grouped = query.reshape(batch, length, KV, HEADS // KV, HD)
    return jnp.einsum(
        "nqgjd,nkgd->ngjqk", grouped, keys, preferred_element_type=jnp.float32
    ) * HD ** (-0.5)


def attend_lines(query, keyval):
    batch, length, feature = query.shape
    keys, values = split_keyval(keyval)
    scores = line_scores(query, keys)
    peak = jnp.max(scores, axis=-1, keepdims=True)
    expon = jnp.exp(scores - peak)
    denominator = jnp.sum(expon, axis=-1)
    mixed = jnp.einsum(
        "ngjqk,nkgd->nqgjd", expon.astype(jnp.bfloat16), values, preferred_element_type=jnp.float32
    )
    mixed = mixed / jnp.transpose(denominator, (0, 3, 1, 2))[..., None]
    return mixed.reshape(batch, length, feature).astype(jnp.bfloat16)


def rms_norm(current, gain):
    values = current.astype(jnp.float32)
    scaled = values * lax.rsqrt(jnp.mean(values * values, axis=-1, keepdims=True) + 1e-06)
    return (scaled * gain).astype(jnp.bfloat16)


def shards(tokens, qkv_weight, out_weight, norm_gain, conv_weight, conv_bias):
    lat_rows, lon_cols, feature = tokens.shape
    widened = with_halo(tokens, (("lon", 1),), 1, True)
    padded = with_halo(widened, (("lat", 0),), 1, False)
    total = tokens.astype(jnp.float32) + conv_bias.astype(jnp.float32)
    for shift_lat in range(3):
        for shift_lon in range(3):
            window = padded[
                shift_lat : shift_lat + lat_rows, shift_lon : shift_lon + lon_cols
            ].astype(jnp.float32)
            total = total + conv_weight[3 * shift_lat + shift_lon].astype(jnp.float32) * window
    current = total.astype(jnp.bfloat16)
    for section_index in range(2):
        weight_in, weight_out = (
            lax.all_gather(qkv_weight[section_index], "lon", axis=1, tiled=True),
            lax.all_gather(out_weight[section_index], "lon", axis=1, tiled=True),
        )
        normed = rms_norm(current, norm_gain[section_index])
        projected = jnp.dot(
            normed.reshape(-1, feature), weight_in, preferred_element_type=jnp.float32
        )
        projected = projected.astype(jnp.bfloat16).reshape(lat_rows, lon_cols, -1)
        query = projected[..., :feature]
        keyval = projected[..., feature:]
        if section_index == 0:
            gathered = lax.all_gather(keyval, "lon", axis=1, tiled=True)
            attended = attend_lines(query, gathered)
        else:
            gathered = lax.all_gather(keyval, "lat", axis=0, tiled=True)
            attended = attend_lines(
                jnp.transpose(query, (1, 0, 2)), jnp.transpose(gathered, (1, 0, 2))
            )
            attended = jnp.transpose(attended, (1, 0, 2))
        output = jnp.dot(
            attended.reshape(-1, feature), weight_out, preferred_element_type=jnp.float32
        )
        current = (
            current.astype(jnp.float32) + output.reshape(lat_rows, lon_cols, feature)
        ).astype(jnp.bfloat16)
    return current


MESH = pl.DeviceIdType.MESH
F32 = jnp.float32
BF16 = jnp.bfloat16
PLANE = 8
UNROLL = 1


def remote(src, dst, send, recv, device):
    return pltpu.make_async_remote_copy(
        src_ref=src, dst_ref=dst, send_sem=send, recv_sem=recv, device_id=device, device_id_type=MESH
    )


def step_kernel(
    nlat, nlon, tokens, wq_in, wo_in, gain, conv_w, conv_b, out,
    wq, wo, pad, edgef, edge, hcol, hrow, hcor, cur, normed, turned, turn, proj, att, kvs, kv0, kv1, kvt,
    sem_w, sem_z, sem_f, sem_c, sem_hs, sem_hr, sem_ks, sem_kr, sem_l,
):
    cols, rows, feature = tokens.shape
    step0, step1, sent = 16, 32, 24
    count = rows * step0
    ens, lat, lon = lax.axis_index("ens"), lax.axis_index("lat"), lax.axis_index("lon")
    here = ens * 4 + lax.rem(lat, 4)

    def flip(value, bit):
        return value + bit - 2 * bit * lax.rem(value // bit, 2)

    wide = wq_in.shape[1]
    piece_q, piece_o = wide // PLANE, feature // PLANE
    dev_core = (ens, flip(lat, 1), lon)
    dev_x = (ens, flip(lat, 2), lon)
    dev_y = (1 - ens, lat, lon)
    dev_xy = (1 - ens, flip(lat, 2), lon)
    p_core, p_x, p_y = flip(here, 1), flip(here, 2), flip(here, 4)
    p_xy = flip(p_x, 4)
    far = [lax.rem(lon + d, nlon) for d in range(nlon)]
    farlat = [lax.rem(lat + d, nlat) for d in range(nlat)]

    def rows_of(m, p):
        size = piece_o if m % 2 else piece_q
        return pl.ds(pl.multiple_of(p * size, size), size)

    def part(m, s, p):
        return (wo if m % 2 else wq).at[m // 2, s, rows_of(m, p), :]

    def own(m):
        return (wo_in if m % 2 else wq_in).at[m // 2]

    cur[...] = jnp.zeros_like(cur)
    normed[...] = jnp.zeros_like(normed)
    kv0[...] = jnp.zeros_like(kv0)
    kv1[...] = jnp.zeros_like(kv1)

    barrier = pltpu.get_barrier_semaphore()
    greet = [(ens, lat, far[d]) for d in range(1, nlon)]
    greet += [(ens, farlat[d], lon) for d in range(1, nlat)]
    greet += [(ens, farlat[a], far[b]) for a in (1, nlat - 1) for b in (1, nlon - 1)]
    greet += [dev_y, dev_xy]
    for device in greet:
        pl.semaphore_signal(barrier, inc=1, device_id=device, device_id_type=MESH)
    pl.semaphore_wait(barrier, len(greet))

    pending, kv_sends = [], []

    def launch(copy):
        copy.start()
        pending.append(copy)

    def send_z(m):
        for d in range(1, nlon):
            launch(remote(
                own(m).at[rows_of(m, here), :],
                part(m, lon, here), sem_z.at[m, d], sem_w.at[m, lon, here], (ens, lat, far[d]),
            ))

    def arrived(m, s, p):
        remote(part(m, s, p), part(m, s, p), sem_z.at[m, 0], sem_w.at[m, s, p], dev_core).wait_recv()

    def pass_on(m, s, p, send, device):
        launch(remote(part(m, s, p), part(m, s, p), send, sem_w.at[m, s, p], device))

    def spread(m):
        for d in (1, 3, 2) if nlon == 4 else range(1, nlon):
            arrived(m, far[d], here)
            pass_on(m, far[d], here, sem_f.at[m, d, 0], dev_x)
            pass_on(m, far[d], here, sem_f.at[m, d, 1], dev_y)
            pass_on(m, far[d], here, sem_f.at[m, d, 3], dev_core)

    def share(m):
        for d in (1, 3, 2) if nlon == 4 else range(1, nlon):
            for k, (p, onward) in enumerate(((p_x, dev_y), (p_y, dev_x))):
                arrived(m, far[d], p)
                if (m + d) % 2 == k:
                    pass_on(m, far[d], p, sem_f.at[m, d, 2], onward)
                pass_on(m, far[d], p, sem_c.at[m, d, k], dev_core)

    def share_diagonal(m):
        for d in (1, 3, 2) if nlon == 4 else range(1, nlon):
            arrived(m, far[d], p_xy)
            pass_on(m, far[d], p_xy, sem_c.at[m, d, 2], dev_core)

    def finish(m):
        pltpu.make_async_copy(own(m), (wo if m % 2 else wq).at[m // 2, lon], sem_l.at[m]).wait()
        for d in range(1, nlon):
            for p in (p_core, flip(p_x, 1), flip(p_y, 1), flip(p_xy, 1)):
                arrived(m, far[d], p)

    send_z(0)
    for m in range(4):
        pltpu.make_async_copy(own(m), (wo if m % 2 else wq).at[m // 2, lon], sem_l.at[m]).start()

    edgef[...] = jnp.zeros_like(edgef)
    for j in range(cols):
        line = tokens[j].astype(F32)
        pad[1 + j, 8 : 8 + rows, :] = line
        edgef[0, j : j + 1, :] = line[0:1]
        edgef[1, j : j + 1, :] = line[rows - 1 : rows]
    edge[...] = edgef[...].astype(BF16)
    north, south, west, east = farlat[nlat - 1], farlat[1], far[nlon - 1], far[1]
    halos = [
        (tokens.at[cols - 1], hcol.at[0], (ens, lat, east)),
        (tokens.at[0], hcol.at[1], (ens, lat, west)),
        (edge.at[1], hrow.at[0], (ens, south, lon)),
        (edge.at[0], hrow.at[1], (ens, north, lon)),
        (edge.at[1], hcor.at[0], (ens, south, east)),
        (edge.at[1], hcor.at[1], (ens, south, west)),
        (edge.at[0], hcor.at[2], (ens, north, east)),
        (edge.at[0], hcor.at[3], (ens, north, west)),
    ]
    hcopies = [remote(a, b, sem_hs.at[k], sem_hr.at[k], dev) for k, (a, b, dev) in enumerate(halos)]
    for copy in hcopies:
        launch(copy)
    for m in (1, 2, 3):
        send_z(m)
    spread(0)
    for copy in hcopies:
        copy.wait_recv()

    for side, place in ((0, 0), (1, 1 + cols)):
        pad[place, 8 : 8 + rows, :] = hcol[side].astype(F32)
    for k, (spot, inside) in enumerate(((7, lat > 0), (8 + rows, lat < nlat - 1))):
        keep = jnp.where(inside, 1.0, 0.0).astype(F32)
        line = hrow[k].astype(F32) * keep
        for j in range(cols):
            pad[1 + j, spot : spot + 1, :] = line[j : j + 1]
        pad[0, spot : spot + 1, :] = hcor[2 * k].astype(F32)[cols - 1 : cols] * keep
        pad[1 + cols, spot : spot + 1, :] = hcor[2 * k + 1].astype(F32)[0:1] * keep

    taps = conv_w[...].astype(F32)
    bias = conv_b[...].astype(F32).reshape(1, feature)
    alive = lax.broadcasted_iota(jnp.int32, (sent, 1), 0) < rows

    def rms(values, k):
        scaled = values * lax.rsqrt(jnp.mean(values * values, axis=-1, keepdims=True) + 1e-06)
        return (scaled * gain[k : k + 1, :]).astype(BF16)

    def conv_line(j, carry):
        total = pad[j + 1, 8 : 8 + sent, :] + bias
        for a in range(3):
            for b in range(3):
                total = total + taps[3 * a + b : 3 * a + b + 1] * pad[j + b, 7 + a : 7 + a + sent, :]
        total = jnp.where(alive, total, 0.0)
        rounded = jnp.concatenate([total, jnp.zeros((step1 - sent, feature), F32)], axis=0).astype(BF16)
        spot = pl.ds(pl.multiple_of(j * step1, step1), step1)
        cur[spot, :] = rounded
        normed[spot, :] = rms(rounded.astype(F32), 0)
        return carry

    lax.fori_loop(0, cols, conv_line, 0)
    to = lax.broadcasted_iota(jnp.int32, (count, count), 0)
    fro = lax.broadcasted_iota(jnp.int32, (count, count), 1)
    turn[0] = jnp.where(
        (fro == lax.rem(to, step0) * step1 + to // step0) & (lax.rem(to, step0) < cols), 1.0, 0.0
    ).astype(BF16)
    turn[1] = jnp.where(
        (fro == lax.rem(to, step1) * step0 + to // step1) & (lax.rem(to, step1) < rows), 1.0, 0.0
    ).astype(BF16)

    def halves(block):
        left = lax.broadcasted_iota(jnp.int32, block.shape, 1) < HD
        swapped = jnp.concatenate([block[:, HD:], block[:, :HD]], axis=1)
        zero = jnp.zeros_like(block)
        first = (jnp.where(left, block, zero), jnp.where(left, zero, swapped))
        second = (jnp.where(left, swapped, zero), jnp.where(left, zero, block))
        return (first, second)

    def attend(keys_of, values_of, width, blocks, step, valid):
        pairs = HEADS // KV // 2
        packed = 2 * width <= 128

        def contract(a, b):
            return lax.dot_general(a, b, (((1,), (1,)), ((), ())), preferred_element_type=F32)

        def body(r, carry):
            spot = pl.ds(pl.multiple_of(r * step, step), step)
            kh, vh = halves(keys_of(spot)), halves(values_of(spot))
            sides = lax.broadcasted_iota(jnp.int32, (width, 2 * HD), 1) < HD
            ones = [jnp.where(sides, 1.0, 0.0).astype(BF16), jnp.where(sides, 0.0, 1.0).astype(BF16)]
            span = 2 * width if packed else width
            lane = lax.broadcasted_iota(jnp.int32, (1, span), 1)
            valid_key = lax.rem(lane, step) < valid
            for g in range(KV):
                base = g * pairs
                query = jnp.concatenate(
                    [proj[spot, (base + p) * 128 : (base + p + 1) * 128] for p in range(pairs)], axis=0
                )
                blend = [jnp.concatenate([vh[g][half], ones[half]], axis=1) for half in range(2)]
                if packed:
                    scores = contract(query, jnp.concatenate(kh[g], axis=0))
                    near = jnp.where(valid_key & (lane < width), scores, -jnp.inf)
                    away = jnp.where(valid_key & (lane >= width), scores, -jnp.inf)
                    peak = jnp.where(
                        lane < width,
                        jnp.max(near, axis=-1, keepdims=True),
                        jnp.max(away, axis=-1, keepdims=True),
                    )
                    expon = jnp.where(valid_key, jnp.exp(jnp.where(valid_key, scores - peak, 0.0)), 0.0)
                    both = jnp.dot(
                        expon.astype(BF16), jnp.concatenate(blend, axis=0), preferred_element_type=F32
                    )
                else:
                    both = None
                    for half in range(2):
                        scores = jnp.where(valid_key, contract(query, kh[g][half]), -jnp.inf)
                        expon = jnp.exp(scores - jnp.max(scores, axis=-1, keepdims=True))
                        term = jnp.dot(expon.astype(BF16), blend[half], preferred_element_type=F32)
                        both = term if both is None else both + term
                mixed = (both[:, : 2 * HD] / both[:, 2 * HD :]).astype(BF16)
                for p in range(pairs):
                    att[spot, (base + p) * 128 : (base + p + 1) * 128] = mixed[p * step : (p + 1) * step]
            return carry

        lax.fori_loop(0, blocks, body, 0, unroll=UNROLL)

    def wide_rows(k, low, high):
        return wq.at[k].reshape(nlon * wide, feature)[low:high, :]

    def many(a, b):
        return lax.dot_general(a, b, (((1,), (1,)), ((), ())), preferred_element_type=F32)

    def query_of(k, source):
        for t in range(0, feature, 256):
            proj[:, t : t + 256] = (many(source[...], wide_rows(k, t, t + 256)) * HD ** (-0.5)).astype(BF16)

    def send_kv(k, kv, targets, mine):
        for copy in kv_sends:
            copy.wait_send()
        kv_sends.clear()
        fresh = many(normed[...], wide_rows(k, feature, feature + 2 * KV * HD)).astype(BF16)
        kvs[...] = fresh.reshape(cols, step1, 2 * KV * HD)
        for d, device in targets:
            copy = remote(
                kvs.at[:, pl.ds(0, sent), :], kv.at[mine, :, pl.ds(0, sent), :],
                sem_ks.at[k, d], sem_kr.at[k, mine], device,
            )
            copy.start()
            kv_sends.append(copy)

    def take_kv(k, kv, sources):
        for s in sources:
            spot = kv.at[s, :, pl.ds(0, sent), :]
            remote(spot, spot, sem_ks.at[k, 0], sem_kr.at[k, s], dev_core).wait_recv()

    def back(k, values, s, width):
        lanes = pl.ds(s * width, width)
        return (cur[:, lanes].astype(F32) + jnp.dot(values, wo[k, s], preferred_element_type=F32)).astype(BF16)

    share(0)
    spread(1)
    share_diagonal(0)
    turned[...] = jnp.dot(turn[0], normed[...], preferred_element_type=F32).astype(BF16)
    share(1)
    finish(0)
    send_kv(0, kv0, [(d, (ens, lat, far[d])) for d in range(1, nlon)], lon)
    query_of(0, turned)
    share_diagonal(1)
    spread(2)
    take_kv(0, kv0, far[1:])
    flat = (count, 2 * KV * HD)
    kv0[lon] = kvs[...]
    for s in range(nlon):
        kvt[s] = jnp.dot(turn[0], kv0[s].reshape(flat), preferred_element_type=F32).astype(BF16)

    def gathered(buffer, parts, low, high):
        return lambda spot: jnp.concatenate([buffer[s, spot, low:high] for s in range(parts)], axis=0)

    def lined(low, high):
        def read(spot):
            j = spot.start // step1
            return jnp.concatenate([kv1[s, j, :, low:high] for s in range(nlat)], axis=0)

        return read

    share(2)
    attend(
        gathered(kvt, nlon, 0, KV * HD), gathered(kvt, nlon, KV * HD, 2 * KV * HD),
        nlon * step0, rows, step0, cols,
    )
    share_diagonal(2)
    spread(3)
    turned[...] = jnp.dot(turn[1], att[...], preferred_element_type=F32).astype(BF16)
    finish(1)
    width = wo.shape[3]
    for s in range(nlon):
        cur[:, s * width : (s + 1) * width] = back(0, turned[...], s, width)

    def norm_row(i, carry):
        spot = pl.ds(pl.multiple_of(i * step1, step1), step1)
        normed[spot, :] = rms(cur[spot, :].astype(F32), 1)
        return carry

    lax.fori_loop(0, count // step1, norm_row, 0)
    finish(2)
    send_kv(1, kv1, [(d, (ens, farlat[d], lon)) for d in range(1, nlat)], lat)
    share(3)
    query_of(1, normed)
    share_diagonal(3)
    take_kv(1, kv1, farlat[1:])
    kv1[lat] = kvs[...]
    attend(lined(0, KV * HD), lined(KV * HD, 2 * KV * HD), nlat * step1, cols, step1, rows)
    finish(3)
    for s in range(nlon):
        done = back(1, att[...], s, width)
        out[:, :, s * width : (s + 1) * width] = done.reshape(cols, step1, width)[:, :rows, :]
    for copy in pending + kv_sends:
        copy.wait_send()


def fused(tokens, qkv_weight, out_weight, norm_gain, conv_weight, conv_bias, nlat, nlon):
    tokens, qkv_weight = jnp.swapaxes(tokens, 0, 1), jnp.swapaxes(qkv_weight, 1, 2)
    cols, rows, feature = tokens.shape
    count = rows * 16
    columns = 2 * KV * HD
    vmem = pl.BlockSpec(memory_space=pltpu.VMEM)
    hbm = pl.BlockSpec(memory_space=pl.ANY)
    dma = pltpu.SemaphoreType.DMA
    result = pl.pallas_call(
        functools.partial(step_kernel, nlat, nlon),
        out_shape=jax.ShapeDtypeStruct(tokens.shape, BF16),
        in_specs=[vmem, hbm, hbm, vmem, vmem, vmem],
        out_specs=vmem,
        scratch_shapes=[
            pltpu.VMEM((2, nlon) + qkv_weight.shape[1:], BF16),
            pltpu.VMEM((2, nlon) + out_weight.shape[1:], BF16),
            pltpu.VMEM((cols + 2, 40, feature), F32),
            pltpu.VMEM((2, 16, feature), F32),
            pltpu.VMEM((2, 16, feature), BF16),
            pltpu.VMEM((2, rows, feature), BF16),
            pltpu.VMEM((2, 16, feature), BF16),
            pltpu.VMEM((4, 16, feature), BF16),
            pltpu.VMEM((count, feature), BF16),
            pltpu.VMEM((count, feature), BF16),
            pltpu.VMEM((count, feature), BF16),
            pltpu.VMEM((2, count, count), BF16),
            pltpu.VMEM((count, feature), BF16),
            pltpu.VMEM((count, feature), BF16),
            pltpu.VMEM((cols, 32, columns), BF16),
            pltpu.VMEM((nlon, cols, 32, columns), BF16),
            pltpu.VMEM((nlat, cols, 32, columns), BF16),
            pltpu.VMEM((nlon, count, columns), BF16),
            dma((4, nlon, PLANE)),
            dma((4, nlon)),
            dma((4, nlon, 4)),
            dma((4, nlon, 3)),
            dma((8,)),
            dma((8,)),
            dma((2, max(nlat, nlon))),
            dma((2, max(nlat, nlon))),
            dma((4,)),
        ],
        compiler_params=pltpu.CompilerParams(
            collective_id=0, has_side_effects=True, vmem_limit_bytes=56 * 2**20
        ),
    )(tokens, qkv_weight, out_weight, norm_gain, conv_weight, conv_bias)
    return jnp.swapaxes(result, 0, 1)


def entry(tokens, qkv_weight, out_weight, norm_gain, conv_weight, conv_bias):
    nens, nlat, nlon = (lax.axis_size(name) for name in ("ens", "lat", "lon"))
    if (nens, nlat, nlon) == (2, 4, 4) and tokens.shape[:2] == (22, 11):
        return fused(
            tokens, qkv_weight, out_weight, norm_gain, conv_weight, conv_bias, nlat, nlon
        )
    return shards(tokens, qkv_weight, out_weight, norm_gain, conv_weight, conv_bias)


def solution(mesh):
    in_specs = (
        P(("ens", "lat"), "lon", None),
        P(None, None, "lon"),
        P(None, None, "lon"),
        P(),
        P(),
        P(),
    )
    out_specs = P(("ens", "lat"), "lon", None)
    return jax.shard_map(entry, mesh=mesh, in_specs=in_specs, out_specs=out_specs, check_vma=False)
```

```python
import functools

import jax
import jax.numpy as jnp
from jax import lax
from jax.experimental import pallas as pl
from jax.experimental.pallas import tpu as pltpu
from jax.sharding import PartitionSpec as P

HEADS = 16
KV = 2
HD = 64


def with_halo(cells, sides, width, closed):
    for axis, dim in sides:
        count = lax.axis_size(axis)
        ends = count if closed else count - 1
        head = lax.slice_in_dim(cells, 0, width, axis=dim)
        tail = lax.slice_in_dim(cells, cells.shape[dim] - width, cells.shape[dim], axis=dim)
        cells = jnp.concatenate(
            [
                lax.ppermute(tail, axis, [(i, (i + 1) % count) for i in range(ends)]),
                cells,
                lax.ppermute(head, axis, [((i + 1) % count, i) for i in range(ends)]),
            ],
            axis=dim,
        )
    return cells


def split_keyval(keyval):
    batch, length, columns = keyval.shape
    keys = keyval[..., : KV * HD].reshape(batch, length, KV, HD)
    values = keyval[..., KV * HD :].reshape(batch, length, KV, HD)
    return (keys, values)


def line_scores(query, keys):
    batch, length, feature = query.shape
    grouped = query.reshape(batch, length, KV, HEADS // KV, HD)
    return jnp.einsum(
        "nqgjd,nkgd->ngjqk", grouped, keys, preferred_element_type=jnp.float32
    ) * HD ** (-0.5)


def attend_lines(query, keyval):
    batch, length, feature = query.shape
    keys, values = split_keyval(keyval)
    scores = line_scores(query, keys)
    peak = jnp.max(scores, axis=-1, keepdims=True)
    expon = jnp.exp(scores - peak)
    denominator = jnp.sum(expon, axis=-1)
    mixed = jnp.einsum(
        "ngjqk,nkgd->nqgjd", expon.astype(jnp.bfloat16), values, preferred_element_type=jnp.float32
    )
    mixed = mixed / jnp.transpose(denominator, (0, 3, 1, 2))[..., None]
    return mixed.reshape(batch, length, feature).astype(jnp.bfloat16)


def rms_norm(current, gain):
    values = current.astype(jnp.float32)
    scaled = values * lax.rsqrt(jnp.mean(values * values, axis=-1, keepdims=True) + 1e-06)
    return (scaled * gain).astype(jnp.bfloat16)


def shards(tokens, qkv_weight, out_weight, norm_gain, conv_weight, conv_bias):
    lat_rows, lon_cols, feature = tokens.shape
    widened = with_halo(tokens, (("lon", 1),), 1, True)
    padded = with_halo(widened, (("lat", 0),), 1, False)
    total = tokens.astype(jnp.float32) + conv_bias.astype(jnp.float32)
    for shift_lat in range(3):
        for shift_lon in range(3):
            window = padded[
                shift_lat : shift_lat + lat_rows, shift_lon : shift_lon + lon_cols
            ].astype(jnp.float32)
            total = total + conv_weight[3 * shift_lat + shift_lon].astype(jnp.float32) * window
    current = total.astype(jnp.bfloat16)
    for section_index in range(2):
        weight_in, weight_out = (
            lax.all_gather(qkv_weight[section_index], "lon", axis=1, tiled=True),
            lax.all_gather(out_weight[section_index], "lon", axis=1, tiled=True),
        )
        normed = rms_norm(current, norm_gain[section_index])
        projected = jnp.dot(
            normed.reshape(-1, feature), weight_in, preferred_element_type=jnp.float32
        )
        projected = projected.astype(jnp.bfloat16).reshape(lat_rows, lon_cols, -1)
        query = projected[..., :feature]
        keyval = projected[..., feature:]
        if section_index == 0:
            gathered = lax.all_gather(keyval, "lon", axis=1, tiled=True)
            attended = attend_lines(query, gathered)
        else:
            gathered = lax.all_gather(keyval, "lat", axis=0, tiled=True)
            attended = attend_lines(
                jnp.transpose(query, (1, 0, 2)), jnp.transpose(gathered, (1, 0, 2))
            )
            attended = jnp.transpose(attended, (1, 0, 2))
        output = jnp.dot(
            attended.reshape(-1, feature), weight_out, preferred_element_type=jnp.float32
        )
        current = (
            current.astype(jnp.float32) + output.reshape(lat_rows, lon_cols, feature)
        ).astype(jnp.bfloat16)
    return current


MESH = pl.DeviceIdType.MESH
F32 = jnp.float32
BF16 = jnp.bfloat16
PLANE = 8
UNROLL0 = 11
UNROLL1 = 11


def remote(src, dst, send, recv, device):
    return pltpu.make_async_remote_copy(
        src_ref=src, dst_ref=dst, send_sem=send, recv_sem=recv, device_id=device, device_id_type=MESH
    )


def step_kernel(
    nlat, nlon, tokens, wq_in, wo_in, gain, conv_w, conv_b, out,
    wq, wo, pad, edgef, edge, hcol, hrow, hcor, cur, normed, turned, turn, proj, att, kvs, kv0, kv1, kvt,
    sem_w, sem_z, sem_f, sem_c, sem_hs, sem_hr, sem_ks, sem_kr, sem_l,
):
    cols, rows, feature = tokens.shape
    step0, step1, sent = 16, 32, 24
    count = rows * step0
    ens, lat, lon = lax.axis_index("ens"), lax.axis_index("lat"), lax.axis_index("lon")
    here = ens * 4 + lax.rem(lat, 4)

    def flip(value, bit):
        return value + bit - 2 * bit * lax.rem(value // bit, 2)

    wide = wq_in.shape[1]
    piece_q, piece_o = wide // PLANE, feature // PLANE
    dev_core = (ens, flip(lat, 1), lon)
    dev_x = (ens, flip(lat, 2), lon)
    dev_y = (1 - ens, lat, lon)
    dev_xy = (1 - ens, flip(lat, 2), lon)
    p_core, p_x, p_y = flip(here, 1), flip(here, 2), flip(here, 4)
    p_xy = flip(p_x, 4)
    far = [lax.rem(lon + d, nlon) for d in range(nlon)]
    farlat = [lax.rem(lat + d, nlat) for d in range(nlat)]

    def rows_of(m, p):
        size = piece_o if m % 2 else piece_q
        return pl.ds(pl.multiple_of(p * size, size), size)

    def part(m, s, p):
        return (wo if m % 2 else wq).at[m // 2, s, rows_of(m, p), :]

    def own(m):
        return (wo_in if m % 2 else wq_in).at[m // 2]

    cur[...] = jnp.zeros_like(cur)
    normed[...] = jnp.zeros_like(normed)
    kv0[...] = jnp.zeros_like(kv0)
    kv1[...] = jnp.zeros_like(kv1)

    barrier = pltpu.get_barrier_semaphore()
    greet = [(ens, lat, far[d]) for d in range(1, nlon)]
    greet += [(ens, farlat[d], lon) for d in range(1, nlat)]
    greet += [(ens, farlat[a], far[b]) for a in (1, nlat - 1) for b in (1, nlon - 1)]
    greet += [dev_y, dev_xy]
    for device in greet:
        pl.semaphore_signal(barrier, inc=1, device_id=device, device_id_type=MESH)
    pl.semaphore_wait(barrier, len(greet))

    pending, kv_sends = [], [[] for g in range(KV)]

    def launch(copy):
        copy.start()
        pending.append(copy)

    def send_z(m):
        for d in range(1, nlon):
            launch(remote(
                own(m).at[rows_of(m, here), :],
                part(m, lon, here), sem_z.at[m, d], sem_w.at[m, lon, here], (ens, lat, far[d]),
            ))

    def arrived(m, s, p):
        remote(part(m, s, p), part(m, s, p), sem_z.at[m, 0], sem_w.at[m, s, p], dev_core).wait_recv()

    def pass_on(m, s, p, send, device):
        launch(remote(part(m, s, p), part(m, s, p), send, sem_w.at[m, s, p], device))

    def spread(m):
        for d in (1, 3, 2) if nlon == 4 else range(1, nlon):
            arrived(m, far[d], here)
            pass_on(m, far[d], here, sem_f.at[m, d, 0], dev_x)
            pass_on(m, far[d], here, sem_f.at[m, d, 1], dev_y)
            pass_on(m, far[d], here, sem_f.at[m, d, 3], dev_core)

    def share(m):
        for d in (1, 3, 2) if nlon == 4 else range(1, nlon):
            for k, (p, onward) in enumerate(((p_x, dev_y), (p_y, dev_x))):
                arrived(m, far[d], p)
                if (m + d) % 2 == k:
                    pass_on(m, far[d], p, sem_f.at[m, d, 2], onward)
                pass_on(m, far[d], p, sem_c.at[m, d, k], dev_core)

    def share_diagonal(m):
        for d in (1, 3, 2) if nlon == 4 else range(1, nlon):
            arrived(m, far[d], p_xy)
            pass_on(m, far[d], p_xy, sem_c.at[m, d, 2], dev_core)

    def finish(m):
        pltpu.make_async_copy(own(m), (wo if m % 2 else wq).at[m // 2, lon], sem_l.at[m]).wait()
        for d in range(1, nlon):
            for p in (p_core, flip(p_x, 1), flip(p_y, 1), flip(p_xy, 1)):
                arrived(m, far[d], p)

    send_z(0)
    for m in range(4):
        pltpu.make_async_copy(own(m), (wo if m % 2 else wq).at[m // 2, lon], sem_l.at[m]).start()

    edgef[...] = jnp.zeros_like(edgef)
    for j in range(cols):
        line = tokens[j].astype(F32)
        pad[1 + j, 8 : 8 + rows, :] = line
        edgef[0, j : j + 1, :] = line[0:1]
        edgef[1, j : j + 1, :] = line[rows - 1 : rows]
    edge[...] = edgef[...].astype(BF16)
    north, south, west, east = farlat[nlat - 1], farlat[1], far[nlon - 1], far[1]
    halos = [
        (tokens.at[cols - 1], hcol.at[0], (ens, lat, east)),
        (tokens.at[0], hcol.at[1], (ens, lat, west)),
        (edge.at[1], hrow.at[0], (ens, south, lon)),
        (edge.at[0], hrow.at[1], (ens, north, lon)),
        (edge.at[1], hcor.at[0], (ens, south, east)),
        (edge.at[1], hcor.at[1], (ens, south, west)),
        (edge.at[0], hcor.at[2], (ens, north, east)),
        (edge.at[0], hcor.at[3], (ens, north, west)),
    ]
    hcopies = [remote(a, b, sem_hs.at[k], sem_hr.at[k], dev) for k, (a, b, dev) in enumerate(halos)]
    for copy in hcopies:
        launch(copy)
    for m in (1, 2, 3):
        send_z(m)
    spread(0)
    for copy in hcopies:
        copy.wait_recv()

    for side, place in ((0, 0), (1, 1 + cols)):
        pad[place, 8 : 8 + rows, :] = hcol[side].astype(F32)
    for k, (spot, inside) in enumerate(((7, lat > 0), (8 + rows, lat < nlat - 1))):
        keep = jnp.where(inside, 1.0, 0.0).astype(F32)
        line = hrow[k].astype(F32) * keep
        for j in range(cols):
            pad[1 + j, spot : spot + 1, :] = line[j : j + 1]
        pad[0, spot : spot + 1, :] = hcor[2 * k].astype(F32)[cols - 1 : cols] * keep
        pad[1 + cols, spot : spot + 1, :] = hcor[2 * k + 1].astype(F32)[0:1] * keep

    taps = conv_w[...].astype(F32)
    bias = conv_b[...].astype(F32).reshape(1, feature)
    alive = lax.broadcasted_iota(jnp.int32, (sent, 1), 0) < rows

    def rms(values, k):
        scaled = values * lax.rsqrt(jnp.mean(values * values, axis=-1, keepdims=True) + 1e-06)
        return (scaled * gain[k : k + 1, :]).astype(BF16)

    def conv_line(j, carry):
        total = pad[j + 1, 8 : 8 + sent, :] + bias
        for a in range(3):
            for b in range(3):
                total = total + taps[3 * a + b : 3 * a + b + 1] * pad[j + b, 7 + a : 7 + a + sent, :]
        total = jnp.where(alive, total, 0.0)
        rounded = jnp.concatenate([total, jnp.zeros((step1 - sent, feature), F32)], axis=0).astype(BF16)
        spot = pl.ds(pl.multiple_of(j * step1, step1), step1)
        cur[spot, :] = rounded
        normed[spot, :] = rms(rounded.astype(F32), 0)
        return carry

    lax.fori_loop(0, cols, conv_line, 0)
    to = lax.broadcasted_iota(jnp.int32, (count, 1), 0)
    fro = lax.broadcasted_iota(jnp.int32, (count, count), 1)
    turn[0] = jnp.where(
        fro == jnp.where(lax.rem(to, step0) < cols, lax.rem(to, step0) * step1 + to // step0, -1), 1.0, 0.0
    ).astype(BF16)
    turn[1] = jnp.where(
        fro == jnp.where(lax.rem(to, step1) < rows, lax.rem(to, step1) * step0 + to // step1, -1), 1.0, 0.0
    ).astype(BF16)

    def halves(block):
        left = lax.broadcasted_iota(jnp.int32, block.shape, 1) < HD
        swapped = jnp.concatenate([block[:, HD:], block[:, :HD]], axis=1)
        zero = jnp.zeros_like(block)
        keys = (jnp.where(left, block, zero), jnp.where(left, zero, swapped))
        values = (jnp.where(left, swapped, zero), jnp.where(left, zero, block))
        return keys, values

    def attend(g, block_of, width, blocks, step, valid):
        pairs = HEADS // KV // 2
        packed = 2 * width <= 128

        def contract(a, b):
            return lax.dot_general(a, b, (((1,), (1,)), ((), ())), preferred_element_type=F32)

        def body(r, carry):
            spot = pl.ds(pl.multiple_of(r * step, step), step)
            kh, vh = halves(block_of(spot))
            sides = lax.broadcasted_iota(jnp.int32, (width, 2 * HD), 1) < HD
            ones = [jnp.where(sides, 1.0, 0.0).astype(BF16), jnp.where(sides, 0.0, 1.0).astype(BF16)]
            span = 2 * width if packed else width
            lane = lax.broadcasted_iota(jnp.int32, (1, span), 1)
            valid_key = lax.rem(lane, step) < valid
            base = g * pairs
            query = jnp.concatenate(
                [proj[spot, (base + p) * 128 : (base + p + 1) * 128] for p in range(pairs)], axis=0
            )
            blend = [jnp.concatenate([vh[half], ones[half]], axis=1) for half in range(2)]
            if packed:
                scores = contract(query, jnp.concatenate(kh, axis=0))
                near = jnp.where(valid_key & (lane < width), scores, -jnp.inf)
                away = jnp.where(valid_key & (lane >= width), scores, -jnp.inf)
                peak = jnp.where(
                    lane < width,
                    jnp.max(near, axis=-1, keepdims=True),
                    jnp.max(away, axis=-1, keepdims=True),
                )
                expon = jnp.where(valid_key, jnp.exp(jnp.where(valid_key, scores - peak, 0.0)), 0.0)
                both = jnp.dot(
                    expon.astype(BF16), jnp.concatenate(blend, axis=0), preferred_element_type=F32
                )
            else:
                both = None
                for half in range(2):
                    scores = jnp.where(valid_key, contract(query, kh[half]), -jnp.inf)
                    expon = jnp.exp(scores - jnp.max(scores, axis=-1, keepdims=True))
                    term = jnp.dot(expon.astype(BF16), blend[half], preferred_element_type=F32)
                    both = term if both is None else both + term
            mixed = (both[:, : 2 * HD] / both[:, 2 * HD :]).astype(BF16)
            for p in range(pairs):
                att[spot, (base + p) * 128 : (base + p + 1) * 128] = mixed[p * step : (p + 1) * step]
            return carry

        lax.fori_loop(0, blocks, body, 0, unroll=UNROLL0 if packed else UNROLL1)

    def wide_rows(k, low, high):
        return wq.at[k].reshape(nlon * wide, feature)[low:high, :]

    def many(a, b):
        return lax.dot_general(a, b, (((1,), (1,)), ((), ())), preferred_element_type=F32)

    def query_of(k, source):
        for t in range(0, feature, 256):
            proj[:, t : t + 256] = (many(source[...], wide_rows(k, t, t + 256)) * HD ** (-0.5)).astype(BF16)

    def send_kv(k, g, kv, targets, mine):
        for copy in kv_sends[g]:
            copy.wait_send()
        kv_sends[g].clear()
        low = feature + g * HD
        both = jnp.concatenate(
            [wide_rows(k, low, low + HD), wide_rows(k, low + KV * HD, low + KV * HD + HD)], axis=0
        )
        kvs[g] = many(normed[...], both).astype(BF16).reshape(cols, step1, 2 * HD)
        for d, device in targets:
            copy = remote(
                kvs.at[g, :, pl.ds(0, sent), :], kv.at[g, mine, :, pl.ds(0, sent), :],
                sem_ks.at[k, g, d], sem_kr.at[k, g, mine], device,
            )
            copy.start()
            kv_sends[g].append(copy)
        kv[g, mine] = kvs[g]

    def take_kv(k, g, kv, sources):
        for s in sources:
            spot = kv.at[g, s, :, pl.ds(0, sent), :]
            remote(spot, spot, sem_ks.at[k, g, 0], sem_kr.at[k, g, s], dev_core).wait_recv()

    def back(k, values, s, width):
        lanes = pl.ds(s * width, width)
        return (cur[:, lanes].astype(F32) + jnp.dot(values, wo[k, s], preferred_element_type=F32)).astype(BF16)

    turned[...] = jnp.dot(turn[0], normed[...], preferred_element_type=F32).astype(BF16)
    share(0)
    spread(1)
    share_diagonal(0)
    finish(0)
    for g in range(KV):
        send_kv(0, g, kv0, [(d, (ens, lat, far[d])) for d in range(1, nlon)], lon)
    spread(2)
    query_of(0, turned)
    share(1)

    def gathered(g):
        return lambda spot: jnp.concatenate([kvt[g, s, spot, :] for s in range(nlon)], axis=0)

    def lined(g):
        def read(spot):
            j = spot.start // step1
            return jnp.concatenate([kv1[g, s, j] for s in range(nlat)], axis=0)

        return read

    for g in range(KV):
        take_kv(0, g, kv0, far[1:])
        for s in range(nlon):
            kvt[g, s] = jnp.dot(
                turn[0], kv0[g, s].reshape(count, 2 * HD), preferred_element_type=F32
            ).astype(BF16)
        attend(g, gathered(g), nlon * step0, rows, step0, cols)
        if g == 0:
            share_diagonal(1)
            share(2)
            spread(3)
    turned[...] = jnp.dot(turn[1], att[...], preferred_element_type=F32).astype(BF16)
    finish(1)
    share_diagonal(2)
    share(3)
    width = wo.shape[3]
    for s in range(nlon):
        cur[:, s * width : (s + 1) * width] = back(0, turned[...], s, width)

    def norm_row(i, carry):
        spot = pl.ds(pl.multiple_of(i * step1, step1), step1)
        normed[spot, :] = rms(cur[spot, :].astype(F32), 1)
        return carry

    lax.fori_loop(0, count // step1, norm_row, 0)
    finish(2)
    for g in range(KV):
        send_kv(1, g, kv1, [(d, (ens, farlat[d], lon)) for d in range(1, nlat)], lat)
    query_of(1, normed)
    share_diagonal(3)
    for g in range(KV):
        take_kv(1, g, kv1, farlat[1:])
        attend(g, lined(g), nlat * step1, cols, step1, rows)
    finish(3)
    for s in range(nlon):
        done = back(1, att[...], s, width)
        out[:, :, s * width : (s + 1) * width] = done.reshape(cols, step1, width)[:, :rows, :]
    for copy in pending + sum(kv_sends, []):
        copy.wait_send()


def fused(tokens, qkv_weight, out_weight, norm_gain, conv_weight, conv_bias, nlat, nlon):
    tokens, qkv_weight = jnp.swapaxes(tokens, 0, 1), jnp.swapaxes(qkv_weight, 1, 2)
    cols, rows, feature = tokens.shape
    count = rows * 16
    vmem = pl.BlockSpec(memory_space=pltpu.VMEM)
    hbm = pl.BlockSpec(memory_space=pl.ANY)
    dma = pltpu.SemaphoreType.DMA
    result = pl.pallas_call(
        functools.partial(step_kernel, nlat, nlon),
        out_shape=jax.ShapeDtypeStruct(tokens.shape, BF16),
        in_specs=[vmem, hbm, hbm, vmem, vmem, vmem],
        out_specs=vmem,
        scratch_shapes=[
            pltpu.VMEM((2, nlon) + qkv_weight.shape[1:], BF16),
            pltpu.VMEM((2, nlon) + out_weight.shape[1:], BF16),
            pltpu.VMEM((cols + 2, 40, feature), F32),
            pltpu.VMEM((2, 16, feature), F32),
            pltpu.VMEM((2, 16, feature), BF16),
            pltpu.VMEM((2, rows, feature), BF16),
            pltpu.VMEM((2, 16, feature), BF16),
            pltpu.VMEM((4, 16, feature), BF16),
            pltpu.VMEM((count, feature), BF16),
            pltpu.VMEM((count, feature), BF16),
            pltpu.VMEM((count, feature), BF16),
            pltpu.VMEM((2, count, count), BF16),
            pltpu.VMEM((count, feature), BF16),
            pltpu.VMEM((count, feature), BF16),
            pltpu.VMEM((KV, cols, 32, 2 * HD), BF16),
            pltpu.VMEM((KV, nlon, cols, 32, 2 * HD), BF16),
            pltpu.VMEM((KV, nlat, cols, 32, 2 * HD), BF16),
            pltpu.VMEM((KV, nlon, count, 2 * HD), BF16),
            dma((4, nlon, PLANE)),
            dma((4, nlon)),
            dma((4, nlon, 4)),
            dma((4, nlon, 3)),
            dma((8,)),
            dma((8,)),
            dma((2, KV, max(nlat, nlon))),
            dma((2, KV, max(nlat, nlon))),
            dma((4,)),
        ],
        compiler_params=pltpu.CompilerParams(
            collective_id=0, has_side_effects=True, vmem_limit_bytes=56 * 2**20
        ),
    )(tokens, qkv_weight, out_weight, norm_gain, conv_weight, conv_bias)
    return jnp.swapaxes(result, 0, 1)


def entry(tokens, qkv_weight, out_weight, norm_gain, conv_weight, conv_bias):
    nens, nlat, nlon = (lax.axis_size(name) for name in ("ens", "lat", "lon"))
    if (nens, nlat, nlon) == (2, 4, 4) and tokens.shape[:2] == (22, 11):
        return fused(
            tokens, qkv_weight, out_weight, norm_gain, conv_weight, conv_bias, nlat, nlon
        )
    return shards(tokens, qkv_weight, out_weight, norm_gain, conv_weight, conv_bias)


def solution(mesh):
    in_specs = (
        P(("ens", "lat"), "lon", None),
        P(None, None, "lon"),
        P(None, None, "lon"),
        P(),
        P(),
        P(),
    )
    out_specs = P(("ens", "lat"), "lon", None)
    return jax.shard_map(entry, mesh=mesh, in_specs=in_specs, out_specs=out_specs, check_vma=False)
```

```python
import functools

import jax
import jax.numpy as jnp
from jax import lax
from jax.experimental import pallas as pl
from jax.experimental.pallas import tpu as pltpu
from jax.sharding import PartitionSpec as P

HEADS = 16
KV = 2
HD = 64


def with_halo(cells, sides, width, closed):
    for axis, dim in sides:
        count = lax.axis_size(axis)
        ends = count if closed else count - 1
        head = lax.slice_in_dim(cells, 0, width, axis=dim)
        tail = lax.slice_in_dim(cells, cells.shape[dim] - width, cells.shape[dim], axis=dim)
        cells = jnp.concatenate(
            [
                lax.ppermute(tail, axis, [(i, (i + 1) % count) for i in range(ends)]),
                cells,
                lax.ppermute(head, axis, [((i + 1) % count, i) for i in range(ends)]),
            ],
            axis=dim,
        )
    return cells


def split_keyval(keyval):
    batch, length, columns = keyval.shape
    keys = keyval[..., : KV * HD].reshape(batch, length, KV, HD)
    values = keyval[..., KV * HD :].reshape(batch, length, KV, HD)
    return (keys, values)


def line_scores(query, keys):
    batch, length, feature = query.shape
    grouped = query.reshape(batch, length, KV, HEADS // KV, HD)
    return jnp.einsum(
        "nqgjd,nkgd->ngjqk", grouped, keys, preferred_element_type=jnp.float32
    ) * HD ** (-0.5)


def attend_lines(query, keyval):
    batch, length, feature = query.shape
    keys, values = split_keyval(keyval)
    scores = line_scores(query, keys)
    peak = jnp.max(scores, axis=-1, keepdims=True)
    expon = jnp.exp(scores - peak)
    denominator = jnp.sum(expon, axis=-1)
    mixed = jnp.einsum(
        "ngjqk,nkgd->nqgjd", expon.astype(jnp.bfloat16), values, preferred_element_type=jnp.float32
    )
    mixed = mixed / jnp.transpose(denominator, (0, 3, 1, 2))[..., None]
    return mixed.reshape(batch, length, feature).astype(jnp.bfloat16)


def rms_norm(current, gain):
    values = current.astype(jnp.float32)
    scaled = values * lax.rsqrt(jnp.mean(values * values, axis=-1, keepdims=True) + 1e-06)
    return (scaled * gain).astype(jnp.bfloat16)


def shards(tokens, qkv_weight, out_weight, norm_gain, conv_weight, conv_bias):
    lat_rows, lon_cols, feature = tokens.shape
    widened = with_halo(tokens, (("lon", 1),), 1, True)
    padded = with_halo(widened, (("lat", 0),), 1, False)
    total = tokens.astype(jnp.float32) + conv_bias.astype(jnp.float32)
    for shift_lat in range(3):
        for shift_lon in range(3):
            window = padded[
                shift_lat : shift_lat + lat_rows, shift_lon : shift_lon + lon_cols
            ].astype(jnp.float32)
            total = total + conv_weight[3 * shift_lat + shift_lon].astype(jnp.float32) * window
    current = total.astype(jnp.bfloat16)
    for section_index in range(2):
        weight_in, weight_out = (
            lax.all_gather(qkv_weight[section_index], "lon", axis=1, tiled=True),
            lax.all_gather(out_weight[section_index], "lon", axis=1, tiled=True),
        )
        normed = rms_norm(current, norm_gain[section_index])
        projected = jnp.dot(
            normed.reshape(-1, feature), weight_in, preferred_element_type=jnp.float32
        )
        projected = projected.astype(jnp.bfloat16).reshape(lat_rows, lon_cols, -1)
        query = projected[..., :feature]
        keyval = projected[..., feature:]
        if section_index == 0:
            gathered = lax.all_gather(keyval, "lon", axis=1, tiled=True)
            attended = attend_lines(query, gathered)
        else:
            gathered = lax.all_gather(keyval, "lat", axis=0, tiled=True)
            attended = attend_lines(
                jnp.transpose(query, (1, 0, 2)), jnp.transpose(gathered, (1, 0, 2))
            )
            attended = jnp.transpose(attended, (1, 0, 2))
        output = jnp.dot(
            attended.reshape(-1, feature), weight_out, preferred_element_type=jnp.float32
        )
        current = (
            current.astype(jnp.float32) + output.reshape(lat_rows, lon_cols, feature)
        ).astype(jnp.bfloat16)
    return current


MESH = pl.DeviceIdType.MESH
F32 = jnp.float32
BF16 = jnp.bfloat16
PLANE = 8
UNROLL0 = 11
UNROLL1 = 11


def remote(src, dst, send, recv, device):
    return pltpu.make_async_remote_copy(
        src_ref=src, dst_ref=dst, send_sem=send, recv_sem=recv, device_id=device, device_id_type=MESH
    )


def step_kernel(
    nlat, nlon, tokens, wq_in, wo_in, gain, conv_w, conv_b, out,
    wq, wo, pad, edgef, edge, hcol, hrow, hcor, cur, normed, turned, turn, proj, att, kvs, kv0, kv1, kvt,
    sem_w, sem_z, sem_f, sem_c, sem_hs, sem_hr, sem_ks, sem_kr, sem_l,
):
    cols, rows, feature = tokens.shape
    step0, step1, sent = 16, 32, 24
    count = rows * step0
    ens, lat, lon = lax.axis_index("ens"), lax.axis_index("lat"), lax.axis_index("lon")
    here = ens * 4 + lax.rem(lat, 4)

    def flip(value, bit):
        return value + bit - 2 * bit * lax.rem(value // bit, 2)

    wide = wq_in.shape[1]
    piece_q, piece_o = wide // PLANE, feature // PLANE
    dev_core = (ens, flip(lat, 1), lon)
    dev_x = (ens, flip(lat, 2), lon)
    dev_y = (1 - ens, lat, lon)
    dev_xy = (1 - ens, flip(lat, 2), lon)
    p_core, p_x, p_y = flip(here, 1), flip(here, 2), flip(here, 4)
    p_xy = flip(p_x, 4)
    far = [lax.rem(lon + d, nlon) for d in range(nlon)]
    farlat = [lax.rem(lat + d, nlat) for d in range(nlat)]

    def rows_of(m, p):
        size = piece_o if m % 2 else piece_q
        return pl.ds(pl.multiple_of(p * size, size), size)

    def part(m, s, p):
        return (wo if m % 2 else wq).at[m // 2, s, rows_of(m, p), :]

    def own(m):
        return (wo_in if m % 2 else wq_in).at[m // 2]

    cur[...] = jnp.zeros_like(cur)
    normed[...] = jnp.zeros_like(normed)
    kv0[...] = jnp.zeros_like(kv0)
    kv1[...] = jnp.zeros_like(kv1)

    barrier = pltpu.get_barrier_semaphore()
    greet = [(ens, lat, far[d]) for d in range(1, nlon)]
    greet += [(ens, farlat[d], lon) for d in range(1, nlat)]
    greet += [(ens, farlat[a], far[b]) for a in (1, nlat - 1) for b in (1, nlon - 1)]
    greet += [dev_y, dev_xy]
    for device in greet:
        pl.semaphore_signal(barrier, inc=1, device_id=device, device_id_type=MESH)
    pl.semaphore_wait(barrier, len(greet))

    pending, kv_sends = [], [[] for g in range(KV)]

    def launch(copy):
        copy.start()
        pending.append(copy)

    def send_z(m):
        for d in range(1, nlon):
            launch(remote(
                own(m).at[rows_of(m, here), :],
                part(m, lon, here), sem_z.at[m, d], sem_w.at[m, lon, here], (ens, lat, far[d]),
            ))

    def arrived(m, s, p):
        remote(part(m, s, p), part(m, s, p), sem_z.at[m, 0], sem_w.at[m, s, p], dev_core).wait_recv()

    def pass_on(m, s, p, send, device):
        launch(remote(part(m, s, p), part(m, s, p), send, sem_w.at[m, s, p], device))

    def spread(m):
        for d in (1, 3, 2) if nlon == 4 else range(1, nlon):
            arrived(m, far[d], here)
            pass_on(m, far[d], here, sem_f.at[m, d, 0], dev_x)
            pass_on(m, far[d], here, sem_f.at[m, d, 1], dev_y)
            pass_on(m, far[d], here, sem_f.at[m, d, 3], dev_core)

    def share(m):
        for d in (1, 3, 2) if nlon == 4 else range(1, nlon):
            for k, (p, onward) in enumerate(((p_x, dev_y), (p_y, dev_x))):
                arrived(m, far[d], p)
                if (m + d) % 2 == k:
                    pass_on(m, far[d], p, sem_f.at[m, d, 2], onward)
                pass_on(m, far[d], p, sem_c.at[m, d, k], dev_core)

    def share_diagonal(m):
        for d in (1, 3, 2) if nlon == 4 else range(1, nlon):
            arrived(m, far[d], p_xy)
            pass_on(m, far[d], p_xy, sem_c.at[m, d, 2], dev_core)

    def finish(m):
        pltpu.make_async_copy(own(m), (wo if m % 2 else wq).at[m // 2, lon], sem_l.at[m]).wait()
        for d in range(1, nlon):
            for p in (p_core, flip(p_x, 1), flip(p_y, 1), flip(p_xy, 1)):
                arrived(m, far[d], p)

    send_z(0)
    for m in range(4):
        pltpu.make_async_copy(own(m), (wo if m % 2 else wq).at[m // 2, lon], sem_l.at[m]).start()

    edgef[...] = jnp.zeros_like(edgef)
    for j in range(cols):
        line = tokens[j].astype(F32)
        pad[1 + j, 8 : 8 + rows, :] = line
        edgef[0, j : j + 1, :] = line[0:1]
        edgef[1, j : j + 1, :] = line[rows - 1 : rows]
    edge[...] = edgef[...].astype(BF16)
    north, south, west, east = farlat[nlat - 1], farlat[1], far[nlon - 1], far[1]
    halos = [
        (tokens.at[cols - 1], hcol.at[0], (ens, lat, east)),
        (tokens.at[0], hcol.at[1], (ens, lat, west)),
        (edge.at[1], hrow.at[0], (ens, south, lon)),
        (edge.at[0], hrow.at[1], (ens, north, lon)),
        (edge.at[1], hcor.at[0], (ens, south, east)),
        (edge.at[1], hcor.at[1], (ens, south, west)),
        (edge.at[0], hcor.at[2], (ens, north, east)),
        (edge.at[0], hcor.at[3], (ens, north, west)),
    ]
    hcopies = [remote(a, b, sem_hs.at[k], sem_hr.at[k], dev) for k, (a, b, dev) in enumerate(halos)]
    for copy in hcopies:
        launch(copy)
    for m in (1, 2, 3):
        send_z(m)
    spread(0)
    for copy in hcopies:
        copy.wait_recv()

    for side, place in ((0, 0), (1, 1 + cols)):
        pad[place, 8 : 8 + rows, :] = hcol[side].astype(F32)
    for k, (spot, inside) in enumerate(((7, lat > 0), (8 + rows, lat < nlat - 1))):
        keep = jnp.where(inside, 1.0, 0.0).astype(F32)
        line = hrow[k].astype(F32) * keep
        for j in range(cols):
            pad[1 + j, spot : spot + 1, :] = line[j : j + 1]
        pad[0, spot : spot + 1, :] = hcor[2 * k].astype(F32)[cols - 1 : cols] * keep
        pad[1 + cols, spot : spot + 1, :] = hcor[2 * k + 1].astype(F32)[0:1] * keep

    taps = conv_w[...].astype(F32)
    bias = conv_b[...].astype(F32).reshape(1, feature)
    alive = lax.broadcasted_iota(jnp.int32, (sent, 1), 0) < rows

    def rms(values, k):
        scaled = values * lax.rsqrt(jnp.mean(values * values, axis=-1, keepdims=True) + 1e-06)
        return (scaled * gain[k : k + 1, :]).astype(BF16)

    def conv_line(j, carry):
        total = pad[j + 1, 8 : 8 + sent, :] + bias
        for a in range(3):
            for b in range(3):
                total = total + taps[3 * a + b : 3 * a + b + 1] * pad[j + b, 7 + a : 7 + a + sent, :]
        total = jnp.where(alive, total, 0.0)
        rounded = jnp.concatenate([total, jnp.zeros((step1 - sent, feature), F32)], axis=0).astype(BF16)
        spot = pl.ds(pl.multiple_of(j * step1, step1), step1)
        cur[spot, :] = rounded
        normed[spot, :] = rms(rounded.astype(F32), 0)
        return carry

    lax.fori_loop(0, cols, conv_line, 0, unroll=True)
    to = lax.broadcasted_iota(jnp.int32, (count, 1), 0)
    fro = lax.broadcasted_iota(jnp.int32, (count, count), 1)
    turn[0] = jnp.where(
        fro == jnp.where(lax.rem(to, step0) < cols, lax.rem(to, step0) * step1 + to // step0, -1), 1.0, 0.0
    ).astype(BF16)
    turn[1] = jnp.where(
        fro == jnp.where(lax.rem(to, step1) < rows, lax.rem(to, step1) * step0 + to // step1, -1), 1.0, 0.0
    ).astype(BF16)

    def halves(block):
        left = lax.broadcasted_iota(jnp.int32, block.shape, 1) < HD
        swapped = jnp.concatenate([block[:, HD:], block[:, :HD]], axis=1)
        zero = jnp.zeros_like(block)
        keys = (jnp.where(left, block, zero), jnp.where(left, zero, swapped))
        values = (jnp.where(left, swapped, zero), jnp.where(left, zero, block))
        return keys, values

    def attend(g, block_of, width, blocks, step, valid):
        pairs = HEADS // KV // 2
        packed = 2 * width <= 128

        def contract(a, b):
            return lax.dot_general(a, b, (((1,), (1,)), ((), ())), preferred_element_type=F32)

        def body(r, carry):
            spot = pl.ds(pl.multiple_of(r * step, step), step)
            kh, vh = halves(block_of(spot))
            sides = lax.broadcasted_iota(jnp.int32, (width, 2 * HD), 1) < HD
            ones = [jnp.where(sides, 1.0, 0.0).astype(BF16), jnp.where(sides, 0.0, 1.0).astype(BF16)]
            span = 2 * width if packed else width
            lane = lax.broadcasted_iota(jnp.int32, (1, span), 1)
            valid_key = lax.rem(lane, step) < valid
            base = g * pairs
            query = jnp.concatenate(
                [proj[spot, (base + p) * 128 : (base + p + 1) * 128] for p in range(pairs)], axis=0
            )
            blend = [jnp.concatenate([vh[half], ones[half]], axis=1) for half in range(2)]
            if packed:
                scores = contract(query, jnp.concatenate(kh, axis=0))
                near = jnp.where(valid_key & (lane < width), scores, -jnp.inf)
                away = jnp.where(valid_key & (lane >= width), scores, -jnp.inf)
                peak = jnp.where(
                    lane < width,
                    jnp.max(near, axis=-1, keepdims=True),
                    jnp.max(away, axis=-1, keepdims=True),
                )
                expon = jnp.where(valid_key, jnp.exp(jnp.where(valid_key, scores - peak, 0.0)), 0.0)
                both = jnp.dot(
                    expon.astype(BF16), jnp.concatenate(blend, axis=0), preferred_element_type=F32
                )
            else:
                both = None
                for half in range(2):
                    scores = jnp.where(valid_key, contract(query, kh[half]), -jnp.inf)
                    expon = jnp.exp(scores - jnp.max(scores, axis=-1, keepdims=True))
                    term = jnp.dot(expon.astype(BF16), blend[half], preferred_element_type=F32)
                    both = term if both is None else both + term
            mixed = (both[:, : 2 * HD] / both[:, 2 * HD :]).astype(BF16)
            for p in range(pairs):
                att[spot, (base + p) * 128 : (base + p + 1) * 128] = mixed[p * step : (p + 1) * step]
            return carry

        lax.fori_loop(0, blocks, body, 0, unroll=UNROLL0 if packed else UNROLL1)

    def wide_rows(k, low, high):
        return wq.at[k].reshape(nlon * wide, feature)[low:high, :]

    def many(a, b):
        return lax.dot_general(a, b, (((1,), (1,)), ((), ())), preferred_element_type=F32)

    def query_of(k, source):
        for t in range(0, feature, 256):
            proj[:, t : t + 256] = (many(source[...], wide_rows(k, t, t + 256)) * HD ** (-0.5)).astype(BF16)

    def send_kv(k, g, kv, targets, mine):
        for copy in kv_sends[g]:
            copy.wait_send()
        kv_sends[g].clear()
        low = feature + g * HD
        both = jnp.concatenate(
            [wide_rows(k, low, low + HD), wide_rows(k, low + KV * HD, low + KV * HD + HD)], axis=0
        )
        kvs[g] = many(normed[...], both).astype(BF16).reshape(cols, step1, 2 * HD)
        for d, device in targets:
            copy = remote(
                kvs.at[g, :, pl.ds(0, sent), :], kv.at[g, mine, :, pl.ds(0, sent), :],
                sem_ks.at[k, g, d], sem_kr.at[k, g, mine], device,
            )
            copy.start()
            kv_sends[g].append(copy)
        kv[g, mine] = kvs[g]

    def take_kv(k, g, kv, sources):
        for s in sources:
            spot = kv.at[g, s, :, pl.ds(0, sent), :]
            remote(spot, spot, sem_ks.at[k, g, 0], sem_kr.at[k, g, s], dev_core).wait_recv()

    def back(k, values, s, width):
        lanes = pl.ds(s * width, width)
        return (cur[:, lanes].astype(F32) + jnp.dot(values, wo[k, s], preferred_element_type=F32)).astype(BF16)

    turned[...] = jnp.dot(turn[0], normed[...], preferred_element_type=F32).astype(BF16)
    share(0)
    spread(1)
    share_diagonal(0)
    share(1)
    finish(0)
    for g in range(KV):
        send_kv(0, g, kv0, [(d, (ens, lat, far[d])) for d in range(1, nlon)], lon)
    spread(2)
    query_of(0, turned)
    share_diagonal(1)

    def gathered(g):
        return lambda spot: jnp.concatenate([kvt[g, s, spot, :] for s in range(nlon)], axis=0)

    def lined(g):
        def read(spot):
            j = spot.start // step1
            return jnp.concatenate([kv1[g, s, j] for s in range(nlat)], axis=0)

        return read

    for g in range(KV):
        take_kv(0, g, kv0, far[1:])
        for s in range(nlon):
            kvt[g, s] = jnp.dot(
                turn[0], kv0[g, s].reshape(count, 2 * HD), preferred_element_type=F32
            ).astype(BF16)
        attend(g, gathered(g), nlon * step0, rows, step0, cols)
        if g == 0:
            share(2)
            spread(3)
    turned[...] = jnp.dot(turn[1], att[...], preferred_element_type=F32).astype(BF16)
    finish(1)
    share_diagonal(2)
    share(3)
    width = wo.shape[3]
    for s in range(nlon):
        cur[:, s * width : (s + 1) * width] = back(0, turned[...], s, width)

    def norm_row(i, carry):
        spot = pl.ds(pl.multiple_of(i * step1, step1), step1)
        normed[spot, :] = rms(cur[spot, :].astype(F32), 1)
        return carry

    lax.fori_loop(0, count // step1, norm_row, 0, unroll=True)
    finish(2)
    for g in range(KV):
        send_kv(1, g, kv1, [(d, (ens, farlat[d], lon)) for d in range(1, nlat)], lat)
    query_of(1, normed)
    share_diagonal(3)
    for g in range(KV):
        take_kv(1, g, kv1, farlat[1:])
        attend(g, lined(g), nlat * step1, cols, step1, rows)
    finish(3)
    for s in range(nlon):
        done = back(1, att[...], s, width)
        out[:, :, s * width : (s + 1) * width] = done.reshape(cols, step1, width)[:, :rows, :]
    for copy in pending + sum(kv_sends, []):
        copy.wait_send()


def fused(tokens, qkv_weight, out_weight, norm_gain, conv_weight, conv_bias, nlat, nlon):
    tokens, qkv_weight = jnp.swapaxes(tokens, 0, 1), jnp.swapaxes(qkv_weight, 1, 2)
    cols, rows, feature = tokens.shape
    count = rows * 16
    vmem = pl.BlockSpec(memory_space=pltpu.VMEM)
    hbm = pl.BlockSpec(memory_space=pl.ANY)
    dma = pltpu.SemaphoreType.DMA
    result = pl.pallas_call(
        functools.partial(step_kernel, nlat, nlon),
        out_shape=jax.ShapeDtypeStruct(tokens.shape, BF16),
        in_specs=[vmem, hbm, hbm, vmem, vmem, vmem],
        out_specs=vmem,
        scratch_shapes=[
            pltpu.VMEM((2, nlon) + qkv_weight.shape[1:], BF16),
            pltpu.VMEM((2, nlon) + out_weight.shape[1:], BF16),
            pltpu.VMEM((cols + 2, 40, feature), F32),
            pltpu.VMEM((2, 16, feature), F32),
            pltpu.VMEM((2, 16, feature), BF16),
            pltpu.VMEM((2, rows, feature), BF16),
            pltpu.VMEM((2, 16, feature), BF16),
            pltpu.VMEM((4, 16, feature), BF16),
            pltpu.VMEM((count, feature), BF16),
            pltpu.VMEM((count, feature), BF16),
            pltpu.VMEM((count, feature), BF16),
            pltpu.VMEM((2, count, count), BF16),
            pltpu.VMEM((count, feature), BF16),
            pltpu.VMEM((count, feature), BF16),
            pltpu.VMEM((KV, cols, 32, 2 * HD), BF16),
            pltpu.VMEM((KV, nlon, cols, 32, 2 * HD), BF16),
            pltpu.VMEM((KV, nlat, cols, 32, 2 * HD), BF16),
            pltpu.VMEM((KV, nlon, count, 2 * HD), BF16),
            dma((4, nlon, PLANE)),
            dma((4, nlon)),
            dma((4, nlon, 4)),
            dma((4, nlon, 3)),
            dma((8,)),
            dma((8,)),
            dma((2, KV, max(nlat, nlon))),
            dma((2, KV, max(nlat, nlon))),
            dma((4,)),
        ],
        compiler_params=pltpu.CompilerParams(
            collective_id=0, has_side_effects=True, vmem_limit_bytes=56 * 2**20
        ),
    )(tokens, qkv_weight, out_weight, norm_gain, conv_weight, conv_bias)
    return jnp.swapaxes(result, 0, 1)


def entry(tokens, qkv_weight, out_weight, norm_gain, conv_weight, conv_bias):
    nens, nlat, nlon = (lax.axis_size(name) for name in ("ens", "lat", "lon"))
    if (nens, nlat, nlon) == (2, 4, 4) and tokens.shape[:2] == (22, 11):
        return fused(
            tokens, qkv_weight, out_weight, norm_gain, conv_weight, conv_bias, nlat, nlon
        )
    return shards(tokens, qkv_weight, out_weight, norm_gain, conv_weight, conv_bias)


def solution(mesh):
    in_specs = (
        P(("ens", "lat"), "lon", None),
        P(None, None, "lon"),
        P(None, None, "lon"),
        P(),
        P(),
        P(),
    )
    out_specs = P(("ens", "lat"), "lon", None)
    return jax.shard_map(entry, mesh=mesh, in_specs=in_specs, out_specs=out_specs, check_vma=False)
```
